1024 devices in a mesh: grp: 64 (over y, x, z_hi), mem: 16 (over z_lo, core).
Axes of the slice: x: 4, y: 4, z: 32 (z_hi: 4, z_lo: 8; z = z_hi * 8 + z_lo), core: 2. Of those that a mesh axis runs over, the one named last changes fastest.
Arguments:
- stem: bfloat16 [2, 64, 16, 1024, 256], P(None, 'grp', 'mem'), may hold values from -6 to 6
- branches: bfloat16 [3, 2, 256, 256], replicated, may hold values from -0.25 to 0.25
- mode_order: int32 [3, 256], replicated, may hold values from 0 to 255, each once within a row
Outputs:
- contracted: bfloat16 [2, 64, 16, 1024, 256], P(None, 'grp', 'mem')
The draws below stay inside these ranges and needn't reach their ends.
Inputs may be any that keep to these rules, and one draw needn't show every extreme that they name: Each row of mode_order names every number below 256 once.
All inputs are finite; a program needn't handle non-finite values.
Results may differ from the reference program's by a relative error of at most 0.0057.
Values may be sent and summed in bfloat16 or wider, within the bound.
A program may use at most 32 MiB of HBM per device.

```python
import jax
import jax.numpy as jnp
from jax import lax

BLOCK = 256
ROWS = 1024
NG = 64
NM = 16
U2 = 16
U3 = 4


def levels(own_key, shape, shards, low, high):
    level, own = 1.0, jax.random.fold_in(own_key, 6)
    for dim, shards_of in shards:
        steps = jnp.exp(jax.random.uniform(jax.random.fold_in(own, dim), (shards_of,), jnp.float32, low / len(shards), high / len(shards)))
        level = level * jnp.repeat(steps, shape[dim] // shards_of).reshape([-1 if axis == dim else 1 for axis in range(len(shape))])
    return level


def centred(own_key, shape, deviation, bound, split=(), dtype=jnp.bfloat16):
    array = deviation * jax.random.normal(own_key, shape, jnp.float32)
    if split:
        array = array * levels(own_key, shape, split, -0.22, 0.18)
    return jnp.clip(array, -bound, bound).astype(dtype)


def setup_inputs(seed: int = 0) -> dict:
    key_list = jax.random.split(jax.random.key(seed), 4)
    return {
        "stem": centred(key_list[0], (2, NG, NM, ROWS, BLOCK), 1.0, 6.0, ((1, 64), (2, 16))),
        "branches": centred(key_list[1], (3, 2, BLOCK, BLOCK), (2 * BLOCK) ** -0.5, 0.25),
        "mode_order": jax.vmap(lambda own: jax.random.permutation(own, BLOCK))(jax.random.split(key_list[2], 3)).reshape((3, BLOCK)).astype(jnp.int32),
    }


def real_matrix(branches, mode_order, section_no):
    weight = branches[section_no][:, mode_order[section_no], :]
    upper = jnp.concatenate([weight[0], weight[1]], axis=1)
    lower = jnp.concatenate([-weight[1], weight[0]], axis=1)
    return jnp.concatenate([upper, lower], axis=0)


def contract(stem_view, branches, mode_order, section_no):
    real_form = real_matrix(branches, mode_order, section_no)

    def one_slab(slab_data):
        joined = jnp.concatenate([slab_data[0], slab_data[1]], axis=-1)
        result = jnp.dot(joined, real_form, preferred_element_type=jnp.float32)
        return jnp.stack([result[..., :BLOCK], result[..., BLOCK:]]).astype(jnp.bfloat16)

    mapped = lax.map(one_slab, jnp.moveaxis(stem_view, 1, 0))
    return jnp.moveaxis(mapped, 0, 1)


def reference(stem, branches, mode_order):
    first = contract(stem, branches, mode_order, 0)
    view_two = first.reshape(2, NG, NM, ROWS, NM, U2).transpose(0, 1, 4, 3, 2, 5).reshape(2, NG, NM, ROWS, BLOCK)
    second = contract(view_two, branches, mode_order, 1)
    view_three = second.reshape(2, NG, NM, ROWS, NG, U3).transpose(0, 4, 2, 3, 1, 5).reshape(2, NG, NM, ROWS, BLOCK)
    return contract(view_three, branches, mode_order, 2)
```

```python
import functools

import jax
import jax.numpy as jnp
from jax import lax
from jax.experimental import pallas as pl
from jax.experimental.pallas import tpu as pltpu
from jax.sharding import PartitionSpec as P

MESH = pl.DeviceIdType.MESH
CHUNKS = 4
NX = 4
NZ = 4


def dot(a, b, contract):
    return lax.dot_general(a, b, ((contract[:1], contract[1:]), ((), ())), preferred_element_type=jnp.float32)


def one_hot(shape, dim, of_other):
    mine = lax.broadcasted_iota(jnp.int32, shape, dim)
    other = lax.broadcasted_iota(jnp.int32, shape, 1 - dim)
    return jnp.where(mine == of_other(other), 1.0, 0.0).astype(jnp.bfloat16)


def kernel(geom, stem_ref, branch_ref, mode_ref, out_ref, w0, w1, w2, first, arr1, sec, xarr, relp, relm, zarr,
           s1, r1, sx, rx, sz, rz, own_sem):
    nm, nxy, nx, nz, chunks = geom
    ny = nxy // nx
    block = stem_ref.shape[2]
    rows = stem_ref.shape[1] // chunks
    u2, u3 = block // nm, block // (nxy * nz)
    half = nxy // 2
    me = lax.axis_index("mem")
    grp = lax.axis_index("grp")
    zh, xy = lax.rem(grp, nz), lax.div(grp, nz)
    yi, xi = lax.div(xy, nx), lax.rem(xy, nx)
    zp, zm, z2 = lax.rem(zh + 1, nz), lax.rem(zh + nz - 1, nz), lax.rem(zh + 2, nz)
    plus, minus = {"grp": xy * nz + zp}, {"grp": xy * nz + zm}

    mem_peers = [lax.rem(me + d, nm) for d in range(1, nm)]
    xy_peers = []
    for d in range(1, nxy):
        dy, dx = d // nx, d % nx
        xy_peers.append(lax.rem(yi + dy, ny) * nx + lax.rem(xi + dx, nx))

    barrier = pltpu.get_barrier_semaphore()
    for peer in mem_peers:
        pl.semaphore_signal(barrier, inc=1, device_id={"mem": peer}, device_id_type=MESH)
    for peer in xy_peers:
        pl.semaphore_signal(barrier, inc=1, device_id={"grp": peer * nz + zh}, device_id_type=MESH)
    for target in (plus, minus):
        pl.semaphore_signal(barrier, inc=1, device_id=target, device_id_type=MESH)

    def natural(k):
        order = mode_ref[pl.ds(k, 1), :]
        hot = jnp.where(lax.broadcasted_iota(jnp.int32, (block, block), 0) == order, 1.0, 0.0).astype(jnp.bfloat16)
        re = dot(branch_ref[k, 0], hot, (0, 0)).astype(jnp.bfloat16)
        im = dot(branch_ref[k, 1], hot, (0, 0)).astype(jnp.bfloat16)
        top = jnp.concatenate([re, -im], axis=1)
        bottom = jnp.concatenate([im, re], axis=1)
        return jnp.concatenate([top, bottom], axis=0)

    full = (2 * block, 2 * block)

    def by_unit(unit):
        def place(p):
            u, c, l = lax.div(p, 2 * unit), lax.rem(lax.div(p, unit), 2), lax.rem(p, unit)
            return c * block + u * unit + l
        return place

    def by_arrival(p):
        l, c = lax.rem(p, u3), lax.rem(lax.div(p, u3), 2)
        src = lax.rem(lax.div(p, 2 * u3), nxy)
        z = lax.div(p, 2 * u3 * nxy)
        return c * block + (src * nz + z) * u3 + l

    w0[...] = dot(one_hot(full, 1, by_unit(u2)), natural(0), (1, 0)).astype(jnp.bfloat16)

    pl.semaphore_wait(barrier, (nm - 1) + (nxy - 1) + 2)

    def remote(src, dst, send, recv, target):
        return pltpu.make_async_remote_copy(src_ref=src, dst_ref=dst, send_sem=send, recv_sem=recv,
                                            device_id=target, device_id_type=MESH)

    def copies_one(c):
        return [remote(first.at[c, peer], arr1.at[c, me], s1.at[c, d], r1.at[c, d], {"mem": peer})
                for d, peer in enumerate(mem_peers)]

    def arrivals_one(c):
        for d in range(nm - 1):
            src = lax.rem(me + nm - (d + 1), nm)
            remote(first.at[c, src], arr1.at[c, src], s1.at[c, d], r1.at[c, d], {"mem": src}).wait_recv()

    def own_one(c):
        return pltpu.make_async_copy(first.at[c, me], arr1.at[c, me], own_sem.at[c, 0])

    def copies_xy(c):
        return [remote(sec.at[c, peer], xarr.at[c, :, xy], sx.at[c, d], rx.at[c, d], {"grp": peer * nz + zh})
                for d, peer in enumerate(xy_peers)]

    def arrivals_xy(c):
        for d in range(nxy - 1):
            dy, dx = (d + 1) // nx, (d + 1) % nx
            src = lax.rem(yi + ny - dy, ny) * nx + lax.rem(xi + nx - dx, nx)
            remote(sec.at[c, src], xarr.at[c, :, src], sx.at[c, d], rx.at[c, d], {"grp": src * nz + zh}).wait_recv()

    def own_xy(c):
        return pltpu.make_async_copy(sec.at[c, xy], xarr.at[c, :, xy], own_sem.at[c, 1])

    low, high = pl.ds(0, half), pl.ds(half, nxy - half)

    def copies_z(c):
        return [
            remote(xarr.at[c, z2, low], relp.at[c], sz.at[c, 0], rz.at[c, 0], plus),
            remote(xarr.at[c, z2, high], relm.at[c], sz.at[c, 1], rz.at[c, 1], minus),
            remote(xarr.at[c, zp], zarr.at[c, zh], sz.at[c, 2], rz.at[c, 2], plus),
            remote(xarr.at[c, zm], zarr.at[c, zh], sz.at[c, 3], rz.at[c, 3], minus),
        ]

    def own_z(c):
        return pltpu.make_async_copy(xarr.at[c, zh], zarr.at[c, zh], own_sem.at[c, 2])

    def copies_on(c):
        return [
            remote(relp.at[c], zarr.at[c, zm, low], sz.at[c, 4], rz.at[c, 4], plus),
            remote(relm.at[c], zarr.at[c, zp, high], sz.at[c, 5], rz.at[c, 5], minus),
        ]

    def arrivals_z(c):
        remote(xarr.at[c, zm], zarr.at[c, zm], sz.at[c, 2], rz.at[c, 2], plus).wait_recv()
        remote(xarr.at[c, zp], zarr.at[c, zp], sz.at[c, 3], rz.at[c, 3], minus).wait_recv()
        remote(relp.at[c], zarr.at[c, z2, low], sz.at[c, 4], rz.at[c, 4], plus).wait_recv()
        remote(relm.at[c], zarr.at[c, z2, high], sz.at[c, 5], rz.at[c, 5], minus).wait_recv()

    def stage_one(c):
        here = pl.ds(c * rows, rows)
        out = dot(w0[:, :block], stem_ref[0, here, :], (1, 1)) + dot(w0[:, block:], stem_ref[1, here, :], (1, 1))
        first[c] = out.astype(jnp.bfloat16).reshape(nm, 2 * u2, rows)
        own_one(c).start()
        for copy in copies_one(c):
            copy.start()

    def stage_two(c):
        own_one(c).wait()
        arrivals_one(c)
        out = dot(w1[...], arr1[c].reshape(2 * block, rows), (1, 0))
        sec[c] = out.astype(jnp.bfloat16).reshape(nxy, nz, 2 * u3, rows)
        own_xy(c).start()
        for copy in copies_xy(c):
            copy.start()

    def stage_z(c):
        own_xy(c).wait()
        arrivals_xy(c)
        for copy in copies_z(c):
            copy.start()
        own_z(c).start()

    def stage_on(c):
        for copy, (buf, i, target) in zip(copies_on(c), ((relp, 0, plus), (relm, 1, minus))):
            remote(buf.at[c], buf.at[c], sz.at[c, i], rz.at[c, i], target).wait_recv()
            copy.start()

    def stage_out(c):
        own_z(c).wait()
        arrivals_z(c)
        out = dot(w2[...], zarr[c].reshape(2 * block, rows), (1, 0))
        turned = jnp.transpose(out).astype(jnp.bfloat16)
        here = pl.ds(c * rows, rows)
        out_ref[0, here, :] = turned[:, :block]
        out_ref[1, here, :] = turned[:, block:]

    for c in range(chunks):
        stage_one(c)
    tmp = dot(one_hot(full, 1, by_unit(u3)), natural(1), (1, 0)).astype(jnp.bfloat16)
    w1[...] = dot(tmp, one_hot(full, 0, by_unit(u2)), (1, 0)).astype(jnp.bfloat16)
    w2[...] = dot(natural(2), one_hot(full, 0, by_arrival), (1, 0)).astype(jnp.bfloat16)
    stages = (stage_two, stage_z, stage_on, stage_out)
    for step in range(chunks + len(stages) - 1):
        for lag, stage in enumerate(stages):
            if 0 <= step - lag < chunks:
                stage(step - lag)
    for c in range(chunks):
        for copy in copies_one(c) + copies_xy(c) + copies_z(c) + copies_on(c):
            copy.wait_send()


def build(geom):
    nm, nxy, nx, nz, chunks = geom

    def local(stem, branches, mode_order):
        stem = stem[:, 0, 0]
        _, row_count, block = stem.shape
        rows = row_count // chunks
        u2, u3 = block // nm, block // (nxy * nz)
        vmem = pl.BlockSpec(memory_space=pltpu.VMEM)
        weight = pltpu.VMEM((2 * block, 2 * block), jnp.bfloat16)
        relay = pltpu.VMEM((chunks, nxy // 2, 2 * u3, rows), jnp.bfloat16)
        out = pl.pallas_call(
            functools.partial(kernel, geom),
            out_shape=jax.ShapeDtypeStruct(stem.shape, jnp.bfloat16),
            in_specs=[vmem] * 3,
            out_specs=vmem,
            scratch_shapes=[
                weight, weight, weight,
                pltpu.VMEM((chunks, nm, 2 * u2, rows), jnp.bfloat16),
                pltpu.VMEM((chunks, nm, 2 * u2, rows), jnp.bfloat16),
                pltpu.VMEM((chunks, nxy, nz, 2 * u3, rows), jnp.bfloat16),
                pltpu.VMEM((chunks, nz, nxy, 2 * u3, rows), jnp.bfloat16),
                relay, relay,
                pltpu.VMEM((chunks, nz, nxy, 2 * u3, rows), jnp.bfloat16),
                pltpu.SemaphoreType.DMA((chunks, nm - 1)),
                pltpu.SemaphoreType.DMA((chunks, nm - 1)),
                pltpu.SemaphoreType.DMA((chunks, nxy - 1)),
                pltpu.SemaphoreType.DMA((chunks, nxy - 1)),
                pltpu.SemaphoreType.DMA((chunks, 6)),
                pltpu.SemaphoreType.DMA((chunks, 6)),
                pltpu.SemaphoreType.DMA((chunks, 3)),
            ],
            compiler_params=pltpu.CompilerParams(
                collective_id=0, has_side_effects=True, vmem_limit_bytes=48 << 20
            ),
        )(stem, branches, mode_order)
        return out.reshape(2, 1, 1, row_count, block)

    return local


def solution(mesh):
    geom = (mesh.shape["mem"], mesh.shape["grp"] // NZ, NX, NZ, CHUNKS)
    in_specs = (P(None, "grp", "mem", None, None), P(), P())
    out_specs = P(None, "grp", "mem", None, None)
    return jax.shard_map(build(geom), mesh=mesh, in_specs=in_specs, out_specs=out_specs, check_vma=False)
```

```python
import functools

import jax
import jax.numpy as jnp
from jax import lax
from jax.experimental import pallas as pl
from jax.experimental.pallas import tpu as pltpu
from jax.sharding import PartitionSpec as P

MESH = pl.DeviceIdType.MESH
CHUNKS = 2
Z_LAG = 1


def MEM_ORDER(nm):
    return list(range(nm // 2, nm)) + list(range(1, nm // 2))


NX = 4
NZ = 4


def dot(a, b, contract):
    return lax.dot_general(a, b, ((contract[:1], contract[1:]), ((), ())), preferred_element_type=jnp.float32)


def one_hot(shape, dim, of_other):
    mine = lax.broadcasted_iota(jnp.int32, shape, dim)
    line = (shape[0], 1) if dim == 1 else (1, shape[1])
    other = of_other(lax.broadcasted_iota(jnp.int32, line, 1 - dim))
    return jnp.where(mine == other, 1.0, 0.0).astype(jnp.bfloat16)


def kernel(geom, stem_hbm, branch_hbm, mode_hbm, out_ref, stem_ref, branch_ref, mode_ref, w0, w1, w2, first, arr1, sec, xarr, relp, relm, zarr,
           s1, r1, sx, rx, sz, rz, own_sem, in_sem):
    nm, nxy, nx, nz, chunks = geom
    ny = nxy // nx
    block = stem_ref.shape[2]
    rows = stem_ref.shape[1] // chunks
    u2, u3 = block // nm, block // (nxy * nz)
    half = nxy // 2
    me = lax.axis_index("mem")
    grp = lax.axis_index("grp")
    zh, xy = lax.rem(grp, nz), lax.div(grp, nz)
    yi, xi = lax.div(xy, nx), lax.rem(xy, nx)
    zp, zm, z2 = lax.rem(zh + 1, nz), lax.rem(zh + nz - 1, nz), lax.rem(zh + 2, nz)
    plus, minus = {"grp": xy * nz + zp}, {"grp": xy * nz + zm}

    def flipped(d):
        bits = [1 << b for b in range(nm.bit_length() - 1) if d & (1 << b)]
        return me + sum(bit * (1 - 2 * lax.rem(lax.div(me, bit), 2)) for bit in bits)

    mem_peers = [flipped(d) for d in MEM_ORDER(nm)]
    xy_peers = []
    for d in range(1, nxy):
        dy, dx = d // nx, d % nx
        xy_peers.append(lax.rem(yi + dy, ny) * nx + lax.rem(xi + dx, nx))

    barrier = pltpu.get_barrier_semaphore()
    for peer in mem_peers:
        pl.semaphore_signal(barrier, inc=1, device_id={"mem": peer}, device_id_type=MESH)
    for peer in xy_peers:
        pl.semaphore_signal(barrier, inc=1, device_id={"grp": peer * nz + zh}, device_id_type=MESH)
    for target in (plus, minus):
        pl.semaphore_signal(barrier, inc=1, device_id=target, device_id_type=MESH)

    fetch_mode = pltpu.make_async_copy(mode_hbm, mode_ref, in_sem.at[0])
    fetch_branch = [pltpu.make_async_copy(branch_hbm.at[k], branch_ref.at[k], in_sem.at[1 + k]) for k in range(3)]
    fetch_stem = [pltpu.make_async_copy(stem_hbm.at[:, pl.ds(c * rows, rows)], stem_ref.at[:, pl.ds(c * rows, rows)],
                                        in_sem.at[4 + c]) for c in range(chunks)]
    fetch_mode.start()
    fetch_branch[0].start()
    for fetch in fetch_stem:
        fetch.start()
    fetch_branch[1].start()
    fetch_branch[2].start()

    def parts(k):
        fetch_branch[k].wait()
        order = mode_ref[pl.ds(k, 1), :]
        hot = jnp.where(lax.broadcasted_iota(jnp.int32, (block, block), 0) == order, 1.0, 0.0).astype(jnp.bfloat16)
        re = dot(branch_ref[k, 0], hot, (0, 0)).astype(jnp.bfloat16)
        im = dot(branch_ref[k, 1], hot, (0, 0)).astype(jnp.bfloat16)
        return re, im

    def natural(k):
        re, im = parts(k)
        top = jnp.concatenate([re, -im], axis=1)
        bottom = jnp.concatenate([im, re], axis=1)
        return jnp.concatenate([top, bottom], axis=0)

    full = (2 * block, 2 * block)

    def by_unit(unit):
        def place(p):
            u, c, l = lax.div(p, 2 * unit), lax.rem(lax.div(p, unit), 2), lax.rem(p, unit)
            return c * block + u * unit + l
        return place

    def by_arrival(p):
        l, c = lax.rem(p, u3), lax.rem(lax.div(p, u3), 2)
        src = lax.rem(lax.div(p, 2 * u3), nxy)
        z = lax.div(p, 2 * u3 * nxy)
        return c * block + (src * nz + z) * u3 + l

    fetch_mode.wait()
    re, im = (part.reshape(nm, u2, block) for part in parts(0))
    w0[:, 0, :, :block] = re
    w0[:, 0, :, block:] = -im
    w0[:, 1, :, :block] = im
    w0[:, 1, :, block:] = re

    pl.semaphore_wait(barrier, (nm - 1) + (nxy - 1) + 2)

    def remote(src, dst, send, recv, target):
        return pltpu.make_async_remote_copy(src_ref=src, dst_ref=dst, send_sem=send, recv_sem=recv,
                                            device_id=target, device_id_type=MESH)

    def copies_one(c):
        return [remote(first.at[c, peer], arr1.at[c, me], s1.at[c, d], r1.at[c, d], {"mem": peer})
                for d, peer in enumerate(mem_peers)]

    def arrivals_one(c):
        for d, src in enumerate(mem_peers):
            remote(first.at[c, src], arr1.at[c, src], s1.at[c, d], r1.at[c, d], {"mem": src}).wait_recv()

    def own_one(c):
        return pltpu.make_async_copy(first.at[c, me], arr1.at[c, me], own_sem.at[c, 0])

    def copies_xy(c):
        return [remote(sec.at[c, peer], xarr.at[c, :, xy], sx.at[c, d], rx.at[c, d], {"grp": peer * nz + zh})
                for d, peer in enumerate(xy_peers)]

    def arrivals_xy(c):
        for d in range(nxy - 1):
            dy, dx = (d + 1) // nx, (d + 1) % nx
            src = lax.rem(yi + ny - dy, ny) * nx + lax.rem(xi + nx - dx, nx)
            remote(sec.at[c, src], xarr.at[c, :, src], sx.at[c, d], rx.at[c, d], {"grp": src * nz + zh}).wait_recv()

    def own_xy(c):
        return pltpu.make_async_copy(sec.at[c, xy], xarr.at[c, :, xy], own_sem.at[c, 1])

    low, high = pl.ds(0, half), pl.ds(half, nxy - half)

    def copies_z(c):
        return [
            remote(xarr.at[c, z2, low], relp.at[c], sz.at[c, 0], rz.at[c, 0], plus),
            remote(xarr.at[c, z2, high], relm.at[c], sz.at[c, 1], rz.at[c, 1], minus),
            remote(xarr.at[c, zp], zarr.at[c, zh], sz.at[c, 2], rz.at[c, 2], plus),
            remote(xarr.at[c, zm], zarr.at[c, zh], sz.at[c, 3], rz.at[c, 3], minus),
        ]

    def own_z(c):
        return pltpu.make_async_copy(xarr.at[c, zh], zarr.at[c, zh], own_sem.at[c, 2])

    def copies_on(c):
        return [
            remote(relp.at[c], zarr.at[c, zm, low], sz.at[c, 4], rz.at[c, 4], plus),
            remote(relm.at[c], zarr.at[c, zp, high], sz.at[c, 5], rz.at[c, 5], minus),
        ]

    def arrivals_z(c):
        remote(xarr.at[c, zm], zarr.at[c, zm], sz.at[c, 2], rz.at[c, 2], plus).wait_recv()
        remote(xarr.at[c, zp], zarr.at[c, zp], sz.at[c, 3], rz.at[c, 3], minus).wait_recv()
        remote(relp.at[c], zarr.at[c, z2, low], sz.at[c, 4], rz.at[c, 4], plus).wait_recv()
        remote(relm.at[c], zarr.at[c, z2, high], sz.at[c, 5], rz.at[c, 5], minus).wait_recv()

    def stage_one(c):
        here = pl.ds(c * rows, rows)
        fetch_stem[c].wait()
        form = w0[...].reshape(full)
        out = dot(form[:, :block], stem_ref[0, here, :], (1, 1)) + dot(form[:, block:], stem_ref[1, here, :], (1, 1))
        first[c] = out.astype(jnp.bfloat16).reshape(nm, 2 * u2, rows)
        own_one(c).start()
        for copy in copies_one(c):
            copy.start()

    def stage_two(c):
        own_one(c).wait()
        arrivals_one(c)
        out = dot(w1[...], arr1[c].reshape(2 * block, rows), (1, 0))
        sec[c] = out.astype(jnp.bfloat16).reshape(nxy, nz, 2 * u3, rows)
        own_xy(c).start()
        for copy in copies_xy(c):
            copy.start()

    def stage_z(c):
        own_xy(c).wait()
        arrivals_xy(c)
        for copy in copies_z(c):
            copy.start()
        own_z(c).start()

    def stage_on(c):
        for copy, (buf, i, target) in zip(copies_on(c), ((relp, 0, plus), (relm, 1, minus))):
            remote(buf.at[c], buf.at[c], sz.at[c, i], rz.at[c, i], target).wait_recv()
            copy.start()

    def stage_out(c):
        own_z(c).wait()
        arrivals_z(c)
        out = dot(w2[...], zarr[c].reshape(2 * block, rows), (1, 0))
        turned = jnp.transpose(out.astype(jnp.bfloat16))
        here = pl.ds(c * rows, rows)
        out_ref[0, here, :] = turned[:, :block]
        out_ref[1, here, :] = turned[:, block:]

    for c in range(chunks):
        stage_one(c)
    tmp = dot(one_hot(full, 1, by_unit(u3)), natural(1), (1, 0)).astype(jnp.bfloat16)
    w1[...] = dot(tmp, one_hot(full, 0, by_unit(u2)), (1, 0)).astype(jnp.bfloat16)
    w2[...] = dot(natural(2), one_hot(full, 0, by_arrival), (1, 0)).astype(jnp.bfloat16)
    done = 0
    for step in range(chunks):
        stage_two(step)
        while done <= step - Z_LAG:
            stage_z(done)
            done += 1
    for c in range(done, chunks):
        stage_z(c)
    for c in range(chunks):
        stage_on(c)
    for c in range(chunks):
        stage_out(c)
    for c in range(chunks):
        for copy in copies_one(c) + copies_xy(c) + copies_z(c) + copies_on(c):
            copy.wait_send()


def build(geom):
    nm, nxy, nx, nz, chunks = geom

    def local(stem, branches, mode_order):
        stem = stem[:, 0, 0]
        _, row_count, block = stem.shape
        rows = row_count // chunks
        u2, u3 = block // nm, block // (nxy * nz)
        vmem = pl.BlockSpec(memory_space=pltpu.VMEM)
        weight = pltpu.VMEM((2 * block, 2 * block), jnp.bfloat16)
        relay = pltpu.VMEM((chunks, nxy // 2, 2 * u3, rows), jnp.bfloat16)
        out = pl.pallas_call(
            functools.partial(kernel, geom),
            out_shape=jax.ShapeDtypeStruct(stem.shape, jnp.bfloat16),
            in_specs=[pl.BlockSpec(memory_space=pl.ANY)] * 3,
            out_specs=vmem,
            scratch_shapes=[
                pltpu.VMEM(stem.shape, jnp.bfloat16),
                pltpu.VMEM(branches.shape, jnp.bfloat16),
                pltpu.VMEM(mode_order.shape, jnp.int32),
                pltpu.VMEM((nm, 2, u2, 2 * block), jnp.bfloat16),
                weight, weight,
                pltpu.VMEM((chunks, nm, 2 * u2, rows), jnp.bfloat16),
                pltpu.VMEM((chunks, nm, 2 * u2, rows), jnp.bfloat16),
                pltpu.VMEM((chunks, nxy, nz, 2 * u3, rows), jnp.bfloat16),
                pltpu.VMEM((chunks, nz, nxy, 2 * u3, rows), jnp.bfloat16),
                relay, relay,
                pltpu.VMEM((chunks, nz, nxy, 2 * u3, rows), jnp.bfloat16),
                pltpu.SemaphoreType.DMA((chunks, nm - 1)),
                pltpu.SemaphoreType.DMA((chunks, nm - 1)),
                pltpu.SemaphoreType.DMA((chunks, nxy - 1)),
                pltpu.SemaphoreType.DMA((chunks, nxy - 1)),
                pltpu.SemaphoreType.DMA((chunks, 6)),
                pltpu.SemaphoreType.DMA((chunks, 6)),
                pltpu.SemaphoreType.DMA((chunks, 3)),
                pltpu.SemaphoreType.DMA((4 + chunks,)),
            ],
            compiler_params=pltpu.CompilerParams(
                collective_id=0, has_side_effects=True
            ),
        )(stem, branches, mode_order)
        return out.reshape(2, 1, 1, row_count, block)

    return local


def solution(mesh):
    geom = (mesh.shape["mem"], mesh.shape["grp"] // NZ, NX, NZ, CHUNKS)
    in_specs = (P(None, "grp", "mem", None, None), P(), P())
    out_specs = P(None, "grp", "mem", None, None)
    return jax.shard_map(build(geom), mesh=mesh, in_specs=in_specs, out_specs=out_specs, check_vma=False)
```

```python
import functools

import jax
import jax.numpy as jnp
from jax import lax
from jax.experimental import pallas as pl
from jax.experimental.pallas import tpu as pltpu
from jax.sharding import PartitionSpec as P

MESH = pl.DeviceIdType.MESH
CHUNKS = 2
Z_LAG = 1


def MEM_ORDER(nm):
    return list(range(nm // 2, nm)) + list(range(nm // 4, nm // 2)) + list(range(1, nm // 4))


NX = 4
NZ = 4


def dot(a, b, contract):
    return lax.dot_general(a, b, ((contract[:1], contract[1:]), ((), ())), preferred_element_type=jnp.float32)


def one_hot(shape, dim, of_other):
    mine = lax.broadcasted_iota(jnp.int32, shape, dim)
    line = (shape[0], 1) if dim == 1 else (1, shape[1])
    other = of_other(lax.broadcasted_iota(jnp.int32, line, 1 - dim))
    return jnp.where(mine == other, 1.0, 0.0).astype(jnp.bfloat16)


def kernel(geom, stem_hbm, branch_hbm, mode_hbm, out_ref, stem_ref, branch_ref, mode_ref, w0, w1, w2, first, arr1, sec, xarr, relp, relm, zarr,
           s1, r1, sx, rx, sz, rz, own_sem, in_sem):
    nm, nxy, nx, nz, chunks = geom
    ny = nxy // nx
    block = stem_ref.shape[2]
    rows = stem_ref.shape[1] // chunks
    u2, u3 = block // nm, block // (nxy * nz)
    half = nxy // 2
    me = lax.axis_index("mem")
    grp = lax.axis_index("grp")
    zh, xy = lax.rem(grp, nz), lax.div(grp, nz)
    yi, xi = lax.div(xy, nx), lax.rem(xy, nx)
    zp, zm, z2 = lax.rem(zh + 1, nz), lax.rem(zh + nz - 1, nz), lax.rem(zh + 2, nz)
    plus, minus = {"grp": xy * nz + zp}, {"grp": xy * nz + zm}

    def flipped(d):
        bits = [1 << b for b in range(nm.bit_length() - 1) if d & (1 << b)]
        return me + sum(bit * (1 - 2 * lax.rem(lax.div(me, bit), 2)) for bit in bits)

    mem_peers = [flipped(d) for d in MEM_ORDER(nm)]
    xy_peers = []
    for d in range(1, nxy):
        dy, dx = d // nx, d % nx
        xy_peers.append(lax.rem(yi + dy, ny) * nx + lax.rem(xi + dx, nx))

    barrier = pltpu.get_barrier_semaphore()
    for peer in mem_peers:
        pl.semaphore_signal(barrier, inc=1, device_id={"mem": peer}, device_id_type=MESH)
    for peer in xy_peers:
        pl.semaphore_signal(barrier, inc=1, device_id={"grp": peer * nz + zh}, device_id_type=MESH)
    for target in (plus, minus):
        pl.semaphore_signal(barrier, inc=1, device_id=target, device_id_type=MESH)

    fetch_mode = pltpu.make_async_copy(mode_hbm, mode_ref, in_sem.at[0])
    fetch_branch = [pltpu.make_async_copy(branch_hbm.at[k], branch_ref.at[k], in_sem.at[1 + k]) for k in range(3)]
    fetch_stem = [pltpu.make_async_copy(stem_hbm.at[:, pl.ds(c * rows, rows)], stem_ref.at[:, pl.ds(c * rows, rows)],
                                        in_sem.at[4 + c]) for c in range(chunks)]
    fetch_mode.start()
    fetch_branch[0].start()
    for fetch in fetch_stem:
        fetch.start()
    fetch_branch[1].start()
    fetch_branch[2].start()

    def parts(k):
        fetch_branch[k].wait()
        order = mode_ref[pl.ds(k, 1), :]
        hot = jnp.where(lax.broadcasted_iota(jnp.int32, (block, block), 0) == order, 1.0, 0.0).astype(jnp.bfloat16)
        re = dot(branch_ref[k, 0], hot, (0, 0)).astype(jnp.bfloat16)
        im = dot(branch_ref[k, 1], hot, (0, 0)).astype(jnp.bfloat16)
        return re, im

    def natural(k):
        re, im = parts(k)
        top = jnp.concatenate([re, -im], axis=1)
        bottom = jnp.concatenate([im, re], axis=1)
        return jnp.concatenate([top, bottom], axis=0)

    full = (2 * block, 2 * block)

    def by_unit(unit):
        def place(p):
            u, c, l = lax.div(p, 2 * unit), lax.rem(lax.div(p, unit), 2), lax.rem(p, unit)
            return c * block + u * unit + l
        return place

    def by_arrival(p):
        l, c = lax.rem(p, u3), lax.rem(lax.div(p, u3), 2)
        src = lax.rem(lax.div(p, 2 * u3), nxy)
        z = lax.div(p, 2 * u3 * nxy)
        return c * block + (src * nz + z) * u3 + l

    fetch_mode.wait()
    re, im = (part.reshape(nm, u2, block) for part in parts(0))
    w0[:, 0, :, :block] = re
    w0[:, 0, :, block:] = -im
    w0[:, 1, :, :block] = im
    w0[:, 1, :, block:] = re

    def remote(src, dst, send, recv, target):
        return pltpu.make_async_remote_copy(src_ref=src, dst_ref=dst, send_sem=send, recv_sem=recv,
                                            device_id=target, device_id_type=MESH)

    def copies_one(c):
        return [remote(first.at[c, peer], arr1.at[c, me], s1.at[c, d], r1.at[c, d], {"mem": peer})
                for d, peer in enumerate(mem_peers)]

    def arrivals_one(c):
        for d, src in enumerate(mem_peers):
            remote(first.at[c, src], arr1.at[c, src], s1.at[c, d], r1.at[c, d], {"mem": src}).wait_recv()

    def own_one(c):
        return pltpu.make_async_copy(first.at[c, me], arr1.at[c, me], own_sem.at[c, 0])

    def copies_xy(c):
        return [remote(sec.at[c, peer], xarr.at[c, :, xy], sx.at[c, d], rx.at[c, d], {"grp": peer * nz + zh})
                for d, peer in enumerate(xy_peers)]

    def arrivals_xy(c):
        for d in range(nxy - 1):
            dy, dx = (d + 1) // nx, (d + 1) % nx
            src = lax.rem(yi + ny - dy, ny) * nx + lax.rem(xi + nx - dx, nx)
            remote(sec.at[c, src], xarr.at[c, :, src], sx.at[c, d], rx.at[c, d], {"grp": src * nz + zh}).wait_recv()

    def own_xy(c):
        return pltpu.make_async_copy(sec.at[c, xy], xarr.at[c, :, xy], own_sem.at[c, 1])

    low, high = pl.ds(0, half), pl.ds(half, nxy - half)

    def copies_z(c):
        return [
            remote(xarr.at[c, z2, low], relp.at[c], sz.at[c, 0], rz.at[c, 0], plus),
            remote(xarr.at[c, z2, high], relm.at[c], sz.at[c, 1], rz.at[c, 1], minus),
            remote(xarr.at[c, zp], zarr.at[c, zh], sz.at[c, 2], rz.at[c, 2], plus),
            remote(xarr.at[c, zm], zarr.at[c, zh], sz.at[c, 3], rz.at[c, 3], minus),
        ]

    def own_z(c):
        return pltpu.make_async_copy(xarr.at[c, zh], zarr.at[c, zh], own_sem.at[c, 2])

    def copies_on(c):
        return [
            remote(relp.at[c], zarr.at[c, zm, low], sz.at[c, 4], rz.at[c, 4], plus),
            remote(relm.at[c], zarr.at[c, zp, high], sz.at[c, 5], rz.at[c, 5], minus),
        ]

    def arrivals_z(c):
        remote(xarr.at[c, zm], zarr.at[c, zm], sz.at[c, 2], rz.at[c, 2], plus).wait_recv()
        remote(xarr.at[c, zp], zarr.at[c, zp], sz.at[c, 3], rz.at[c, 3], minus).wait_recv()
        remote(relp.at[c], zarr.at[c, z2, low], sz.at[c, 4], rz.at[c, 4], plus).wait_recv()
        remote(relm.at[c], zarr.at[c, z2, high], sz.at[c, 5], rz.at[c, 5], minus).wait_recv()

    def stage_one(c):
        here = pl.ds(c * rows, rows)
        fetch_stem[c].wait()
        form = w0[...].reshape(full)
        out = dot(form[:, :block], stem_ref[0, here, :], (1, 1)) + dot(form[:, block:], stem_ref[1, here, :], (1, 1))
        first[c] = out.astype(jnp.bfloat16).reshape(nm, 2 * u2, rows)

    def send_one(c):
        for copy in copies_one(c):
            copy.start()
        own_one(c).start()

    def stage_two(c):
        own_one(c).wait()
        arrivals_one(c)
        out = dot(w1[...], arr1[c].reshape(2 * block, rows), (1, 0))
        sec[c] = out.astype(jnp.bfloat16).reshape(nxy, nz, 2 * u3, rows)
        own_xy(c).start()
        for copy in copies_xy(c):
            copy.start()

    def stage_z(c):
        own_xy(c).wait()
        arrivals_xy(c)
        relay_plus, relay_minus, direct_plus, direct_minus = copies_z(c)
        for early, relay, direct in ((zh == nz - 1, relay_plus, direct_plus), (zh == 1, relay_minus, direct_minus)):
            @pl.when(early)
            def _(relay=relay, direct=direct):
                direct.start()
                relay.start()

            @pl.when(jnp.logical_not(early))
            def _(relay=relay, direct=direct):
                relay.start()
                direct.start()
        own_z(c).start()

    def stage_on(c):
        for copy, (buf, i, target) in zip(copies_on(c), ((relp, 0, plus), (relm, 1, minus))):
            remote(buf.at[c], buf.at[c], sz.at[c, i], rz.at[c, i], target).wait_recv()
            copy.start()

    def stage_out(c):
        own_z(c).wait()
        arrivals_z(c)
        out = dot(w2[...], zarr[c].reshape(2 * block, rows), (1, 0))
        turned = jnp.transpose(out.astype(jnp.bfloat16))
        here = pl.ds(c * rows, rows)
        out_ref[0, here, :] = turned[:, :block]
        out_ref[1, here, :] = turned[:, block:]

    for c in range(chunks):
        stage_one(c)
    pl.semaphore_wait(barrier, (nm - 1) + (nxy - 1) + 2)
    for c in range(chunks):
        send_one(c)
    tmp = dot(one_hot(full, 1, by_unit(u3)), natural(1), (1, 0)).astype(jnp.bfloat16)
    w1[...] = dot(tmp, one_hot(full, 0, by_unit(u2)), (1, 0)).astype(jnp.bfloat16)
    w2[...] = dot(natural(2), one_hot(full, 0, by_arrival), (1, 0)).astype(jnp.bfloat16)
    done = 0
    for step in range(chunks):
        stage_two(step)
        while done <= step - Z_LAG:
            stage_z(done)
            done += 1
    for c in range(done, chunks):
        stage_z(c)
    for c in range(chunks):
        stage_on(c)
    for c in range(chunks):
        stage_out(c)
    for c in range(chunks):
        for copy in copies_one(c) + copies_xy(c) + copies_z(c) + copies_on(c):
            copy.wait_send()


def build(geom):
    nm, nxy, nx, nz, chunks = geom

    def local(stem, branches, mode_order):
        stem = stem[:, 0, 0]
        _, row_count, block = stem.shape
        rows = row_count // chunks
        u2, u3 = block // nm, block // (nxy * nz)
        vmem = pl.BlockSpec(memory_space=pltpu.VMEM)
        weight = pltpu.VMEM((2 * block, 2 * block), jnp.bfloat16)
        relay = pltpu.VMEM((chunks, nxy // 2, 2 * u3, rows), jnp.bfloat16)
        out = pl.pallas_call(
            functools.partial(kernel, geom),
            out_shape=jax.ShapeDtypeStruct(stem.shape, jnp.bfloat16),
            in_specs=[pl.BlockSpec(memory_space=pl.ANY)] * 3,
            out_specs=vmem,
            scratch_shapes=[
                pltpu.VMEM(stem.shape, jnp.bfloat16),
                pltpu.VMEM(branches.shape, jnp.bfloat16),
                pltpu.VMEM(mode_order.shape, jnp.int32),
                pltpu.VMEM((nm, 2, u2, 2 * block), jnp.bfloat16),
                weight, weight,
                pltpu.VMEM((chunks, nm, 2 * u2, rows), jnp.bfloat16),
                pltpu.VMEM((chunks, nm, 2 * u2, rows), jnp.bfloat16),
                pltpu.VMEM((chunks, nxy, nz, 2 * u3, rows), jnp.bfloat16),
                pltpu.VMEM((chunks, nz, nxy, 2 * u3, rows), jnp.bfloat16),
                relay, relay,
                pltpu.VMEM((chunks, nz, nxy, 2 * u3, rows), jnp.bfloat16),
                pltpu.SemaphoreType.DMA((chunks, nm - 1)),
                pltpu.SemaphoreType.DMA((chunks, nm - 1)),
                pltpu.SemaphoreType.DMA((chunks, nxy - 1)),
                pltpu.SemaphoreType.DMA((chunks, nxy - 1)),
                pltpu.SemaphoreType.DMA((chunks, 6)),
                pltpu.SemaphoreType.DMA((chunks, 6)),
                pltpu.SemaphoreType.DMA((chunks, 3)),
                pltpu.SemaphoreType.DMA((4 + chunks,)),
            ],
            compiler_params=pltpu.CompilerParams(
                collective_id=0, has_side_effects=True
            ),
        )(stem, branches, mode_order)
        return out.reshape(2, 1, 1, row_count, block)

    return local


def solution(mesh):
    geom = (mesh.shape["mem"], mesh.shape["grp"] // NZ, NX, NZ, CHUNKS)
    in_specs = (P(None, "grp", "mem", None, None), P(), P())
    out_specs = P(None, "grp", "mem", None, None)
    return jax.shard_map(build(geom), mesh=mesh, in_specs=in_specs, out_specs=out_specs, check_vma=False)
```

```python
import functools

import jax
import jax.numpy as jnp
from jax import lax
from jax.experimental import pallas as pl
from jax.experimental.pallas import tpu as pltpu
from jax.sharding import PartitionSpec as P

MESH = pl.DeviceIdType.MESH
CHUNKS = 2
Z_LAG = 1


def MEM_ORDER(nm):
    return list(range(nm // 2, nm)) + list(range(nm // 4, nm // 2)) + list(range(1, nm // 4))


NX = 4
NZ = 4


def dot(a, b, contract):
    return lax.dot_general(a, b, ((contract[:1], contract[1:]), ((), ())), preferred_element_type=jnp.float32)


def one_hot(shape, dim, of_other):
    mine = lax.broadcasted_iota(jnp.int32, shape, dim)
    line = (shape[0], 1) if dim == 1 else (1, shape[1])
    other = of_other(lax.broadcasted_iota(jnp.int32, line, 1 - dim))
    return jnp.where(mine == other, 1.0, 0.0).astype(jnp.bfloat16)


def kernel(geom, stem_hbm, branch_hbm, mode_hbm, out_ref, stem_ref, branch_ref, mode_ref, w0, w1, w2, first, arr1, sec, xarr, relp, relm, zarr,
           s1, r1, sx, rx, sz, rz, own_sem, in_sem):
    nm, nxy, nx, nz, chunks = geom
    ny = nxy // nx
    block = stem_ref.shape[2]
    rows = stem_ref.shape[1] // chunks
    u2, u3 = block // nm, block // (nxy * nz)
    half = nxy // 2
    me = lax.axis_index("mem")
    grp = lax.axis_index("grp")
    zh, xy = lax.rem(grp, nz), lax.div(grp, nz)
    yi, xi = lax.div(xy, nx), lax.rem(xy, nx)
    zp, zm, z2 = lax.rem(zh + 1, nz), lax.rem(zh + nz - 1, nz), lax.rem(zh + 2, nz)
    plus, minus = {"grp": xy * nz + zp}, {"grp": xy * nz + zm}

    def flipped(d):
        bits = [1 << b for b in range(nm.bit_length() - 1) if d & (1 << b)]
        return me + sum(bit * (1 - 2 * lax.rem(lax.div(me, bit), 2)) for bit in bits)

    mem_peers = [flipped(d) for d in MEM_ORDER(nm)]
    xy_peers = []
    for d in range(1, nxy):
        dy, dx = d // nx, d % nx
        xy_peers.append(lax.rem(yi + dy, ny) * nx + lax.rem(xi + dx, nx))

    barrier = pltpu.get_barrier_semaphore()
    for target in (plus, minus):
        pl.semaphore_signal(barrier, inc=1, device_id=target, device_id_type=MESH)
    for peer in mem_peers:
        pl.semaphore_signal(barrier, inc=1, device_id={"mem": peer}, device_id_type=MESH)
    for peer in xy_peers:
        pl.semaphore_signal(barrier, inc=1, device_id={"grp": peer * nz + zh}, device_id_type=MESH)

    fetch_mode = pltpu.make_async_copy(mode_hbm, mode_ref, in_sem.at[0])
    fetch_branch = [pltpu.make_async_copy(branch_hbm.at[k], branch_ref.at[k], in_sem.at[1 + k]) for k in range(3)]
    fetch_stem = [pltpu.make_async_copy(stem_hbm.at[:, pl.ds(c * rows, rows)], stem_ref.at[:, pl.ds(c * rows, rows)],
                                        in_sem.at[4 + c]) for c in range(chunks)]
    fetch_mode.start()
    fetch_branch[0].start()
    for fetch in fetch_stem:
        fetch.start()
    fetch_branch[1].start()
    fetch_branch[2].start()

    def parts(k):
        fetch_branch[k].wait()
        order = mode_ref[pl.ds(k, 1), :]
        hot = jnp.where(lax.broadcasted_iota(jnp.int32, (block, block), 0) == order, 1.0, 0.0).astype(jnp.bfloat16)
        re = dot(branch_ref[k, 0], hot, (0, 0)).astype(jnp.bfloat16)
        im = dot(branch_ref[k, 1], hot, (0, 0)).astype(jnp.bfloat16)
        return re, im

    def natural(k):
        re, im = parts(k)
        top = jnp.concatenate([re, -im], axis=1)
        bottom = jnp.concatenate([im, re], axis=1)
        return jnp.concatenate([top, bottom], axis=0)

    full = (2 * block, 2 * block)

    def by_unit(unit):
        def place(p):
            u, c, l = lax.div(p, 2 * unit), lax.rem(lax.div(p, unit), 2), lax.rem(p, unit)
            return c * block + u * unit + l
        return place

    def by_arrival(p):
        l, c = lax.rem(p, u3), lax.rem(lax.div(p, u3), 2)
        src = lax.rem(lax.div(p, 2 * u3), nxy)
        z = lax.div(p, 2 * u3 * nxy)
        return c * block + (src * nz + z) * u3 + l

    fetch_mode.wait()
    re, im = (part.reshape(nm, u2, block) for part in parts(0))
    w0[:, 0, :, :block] = re
    w0[:, 0, :, block:] = -im
    w0[:, 1, :, :block] = im
    w0[:, 1, :, block:] = re

    def remote(src, dst, send, recv, target):
        return pltpu.make_async_remote_copy(src_ref=src, dst_ref=dst, send_sem=send, recv_sem=recv,
                                            device_id=target, device_id_type=MESH)

    def copies_one(c):
        return [remote(first.at[c, peer], arr1.at[c, me], s1.at[c, d], r1.at[c, d], {"mem": peer})
                for d, peer in enumerate(mem_peers)]

    def arrivals_one(c):
        for d, src in enumerate(mem_peers):
            remote(first.at[c, src], arr1.at[c, src], s1.at[c, d], r1.at[c, d], {"mem": src}).wait_recv()

    def own_one(c):
        return pltpu.make_async_copy(first.at[c, me], arr1.at[c, me], own_sem.at[c, 0])

    def copies_xy(c):
        return [remote(sec.at[c, peer], xarr.at[c, :, xy], sx.at[c, d], rx.at[c, d], {"grp": peer * nz + zh})
                for d, peer in enumerate(xy_peers)]

    def arrivals_xy(c):
        for d in range(nxy - 1):
            dy, dx = (d + 1) // nx, (d + 1) % nx
            src = lax.rem(yi + ny - dy, ny) * nx + lax.rem(xi + nx - dx, nx)
            remote(sec.at[c, src], xarr.at[c, :, src], sx.at[c, d], rx.at[c, d], {"grp": src * nz + zh}).wait_recv()

    def own_xy(c):
        return pltpu.make_async_copy(sec.at[c, xy], xarr.at[c, :, xy], own_sem.at[c, 1])

    low, high = pl.ds(0, half), pl.ds(half, nxy - half)

    def copies_z(c):
        return [
            remote(xarr.at[c, z2, low], relp.at[c], sz.at[c, 0], rz.at[c, 0], plus),
            remote(xarr.at[c, z2, high], relm.at[c], sz.at[c, 1], rz.at[c, 1], minus),
            remote(xarr.at[c, zp], zarr.at[c, zh], sz.at[c, 2], rz.at[c, 2], plus),
            remote(xarr.at[c, zm], zarr.at[c, zh], sz.at[c, 3], rz.at[c, 3], minus),
        ]

    def own_z(c):
        return pltpu.make_async_copy(xarr.at[c, zh], zarr.at[c, zh], own_sem.at[c, 2])

    def copies_on(c):
        return [
            remote(relp.at[c], zarr.at[c, zm, low], sz.at[c, 4], rz.at[c, 4], plus),
            remote(relm.at[c], zarr.at[c, zp, high], sz.at[c, 5], rz.at[c, 5], minus),
        ]

    def arrivals_z(c):
        remote(xarr.at[c, zm], zarr.at[c, zm], sz.at[c, 2], rz.at[c, 2], plus).wait_recv()
        remote(xarr.at[c, zp], zarr.at[c, zp], sz.at[c, 3], rz.at[c, 3], minus).wait_recv()
        remote(relp.at[c], zarr.at[c, z2, low], sz.at[c, 4], rz.at[c, 4], plus).wait_recv()
        remote(relm.at[c], zarr.at[c, z2, high], sz.at[c, 5], rz.at[c, 5], minus).wait_recv()

    def stage_one(c):
        here = pl.ds(c * rows, rows)
        fetch_stem[c].wait()
        form = w0[...].reshape(full)
        out = dot(form[:, :block], stem_ref[0, here, :], (1, 1)) + dot(form[:, block:], stem_ref[1, here, :], (1, 1))
        first[c] = out.astype(jnp.bfloat16).reshape(nm, 2 * u2, rows)

    def send_one(c):
        for copy in copies_one(c):
            copy.start()
        own_one(c).start()

    def stage_two(c):
        own_one(c).wait()
        arrivals_one(c)
        out = dot(w1[...], arr1[c].reshape(2 * block, rows), (1, 0))
        sec[c] = out.astype(jnp.bfloat16).reshape(nxy, nz, 2 * u3, rows)
        own_xy(c).start()
        for copy in copies_xy(c):
            copy.start()

    def stage_z(c):
        own_xy(c).wait()
        arrivals_xy(c)
        relay_plus, relay_minus, direct_plus, direct_minus = copies_z(c)
        for early, relay, direct in ((zh == nz - 1, relay_plus, direct_plus), (zh == 1, relay_minus, direct_minus)):
            @pl.when(early)
            def _(relay=relay, direct=direct):
                direct.start()
                relay.start()

            @pl.when(jnp.logical_not(early))
            def _(relay=relay, direct=direct):
                relay.start()
                direct.start()
        own_z(c).start()

    def stage_on(c):
        for copy, (buf, i, target) in zip(copies_on(c), ((relp, 0, plus), (relm, 1, minus))):
            remote(buf.at[c], buf.at[c], sz.at[c, i], rz.at[c, i], target).wait_recv()
            copy.start()

    def stage_out(c):
        own_z(c).wait()
        arrivals_z(c)
        out = dot(w2[...], zarr[c].reshape(2 * block, rows), (1, 0))
        turned = jnp.transpose(out.astype(jnp.bfloat16))
        here = pl.ds(c * rows, rows)
        out_ref[0, here, :] = turned[:, :block]
        out_ref[1, here, :] = turned[:, block:]

    for c in range(chunks):
        stage_one(c)
    pl.semaphore_wait(barrier, (nm - 1) + (nxy - 1) + 2)
    for c in range(chunks):
        send_one(c)
    tmp = dot(one_hot(full, 1, by_unit(u3)), natural(1), (1, 0)).astype(jnp.bfloat16)
    w1[...] = dot(tmp, one_hot(full, 0, by_unit(u2)), (1, 0)).astype(jnp.bfloat16)
    w2[...] = dot(natural(2), one_hot(full, 0, by_arrival), (1, 0)).astype(jnp.bfloat16)
    done = 0
    for step in range(chunks):
        stage_two(step)
        while done <= step - Z_LAG:
            stage_z(done)
            done += 1
    for c in range(done, chunks):
        stage_z(c)
    for c in range(chunks):
        stage_on(c)
    for c in range(chunks):
        stage_out(c)
    for c in range(chunks):
        for copy in copies_one(c) + copies_xy(c) + copies_z(c) + copies_on(c):
            copy.wait_send()


def build(geom):
    nm, nxy, nx, nz, chunks = geom

    def local(stem, branches, mode_order):
        stem = stem[:, 0, 0]
        _, row_count, block = stem.shape
        rows = row_count // chunks
        u2, u3 = block // nm, block // (nxy * nz)
        vmem = pl.BlockSpec(memory_space=pltpu.VMEM)
        weight = pltpu.VMEM((2 * block, 2 * block), jnp.bfloat16)
        relay = pltpu.VMEM((chunks, nxy // 2, 2 * u3, rows), jnp.bfloat16)
        out = pl.pallas_call(
            functools.partial(kernel, geom),
            out_shape=jax.ShapeDtypeStruct(stem.shape, jnp.bfloat16),
            in_specs=[pl.BlockSpec(memory_space=pl.ANY)] * 3,
            out_specs=vmem,
            scratch_shapes=[
                pltpu.VMEM(stem.shape, jnp.bfloat16),
                pltpu.VMEM(branches.shape, jnp.bfloat16),
                pltpu.VMEM(mode_order.shape, jnp.int32),
                pltpu.VMEM((nm, 2, u2, 2 * block), jnp.bfloat16),
                weight, weight,
                pltpu.VMEM((chunks, nm, 2 * u2, rows), jnp.bfloat16),
                pltpu.VMEM((chunks, nm, 2 * u2, rows), jnp.bfloat16),
                pltpu.VMEM((chunks, nxy, nz, 2 * u3, rows), jnp.bfloat16),
                pltpu.VMEM((chunks, nz, nxy, 2 * u3, rows), jnp.bfloat16),
                relay, relay,
                pltpu.VMEM((chunks, nz, nxy, 2 * u3, rows), jnp.bfloat16),
                pltpu.SemaphoreType.DMA((chunks, nm - 1)),
                pltpu.SemaphoreType.DMA((chunks, nm - 1)),
                pltpu.SemaphoreType.DMA((chunks, nxy - 1)),
                pltpu.SemaphoreType.DMA((chunks, nxy - 1)),
                pltpu.SemaphoreType.DMA((chunks, 6)),
                pltpu.SemaphoreType.DMA((chunks, 6)),
                pltpu.SemaphoreType.DMA((chunks, 3)),
                pltpu.SemaphoreType.DMA((4 + chunks,)),
            ],
            compiler_params=pltpu.CompilerParams(
                collective_id=0, has_side_effects=True
            ),
        )(stem, branches, mode_order)
        return out.reshape(2, 1, 1, row_count, block)

    return local


def solution(mesh):
    geom = (mesh.shape["mem"], mesh.shape["grp"] // NZ, NX, NZ, CHUNKS)
    in_specs = (P(None, "grp", "mem", None, None), P(), P())
    out_specs = P(None, "grp", "mem", None, None)
    return jax.shard_map(build(geom), mesh=mesh, in_specs=in_specs, out_specs=out_specs, check_vma=False)
```
